1024 devices in a mesh: dp: 64 (over x, z_hi, y), tensor: 16 (over z_lo, core).
Axes of the slice: x: 4, y: 8, z: 16 (z_hi: 2, z_lo: 8; z = z_hi * 8 + z_lo), core: 2. Of those that a mesh axis runs over, the one named last changes fastest.
Arguments:
- activations: bfloat16 [8192, 8192], P('dp', 'tensor'), may hold values from -6 to 6
- projection: bfloat16 [8192, 128], replicated, may hold values from -0.5 to 0.5
- grad_gate: bfloat16 [8192, 28672], P('dp', 'tensor'), may hold values from -0.0078125 to 0.0078125
- grad_up: bfloat16 [8192, 28672], P('dp', 'tensor'), may hold values from -0.0078125 to 0.0078125
- first_moment: float32 [128, 2, 28672], P('dp', None, 'tensor'), may hold values from -0.625 to 0.625
- second_moment: float32 [128, 2, 28672], P('dp', None, 'tensor'), may hold values from 0.05 to 0.5
Outputs:
- gate_update: bfloat16 [8192, 28672], P('dp', 'tensor')
- up_update: bfloat16 [8192, 28672], P('dp', 'tensor')
- new_first: float32 [128, 2, 28672], P('dp', None, 'tensor')
- new_second: float32 [128, 2, 28672], P('dp', None, 'tensor')
The draws below stay inside these ranges and needn't reach their ends.
All inputs are finite; a program needn't handle non-finite values.
Results may differ from the reference program's by a relative error of at most 0.015.
Values may be sent and summed in bfloat16 or wider, within the bound.
A program may use at most 32 MiB of HBM per device.

```python
import math
import jax
import jax.numpy as jnp
from jax import lax

D = 8192
RANK = 128
TOK_DEV = 128
STEP = 1000
FF = 28672
TOKENS = 8192
N_DP = 64
N_TENSOR = 16


def steps_of(rng, extent, cuts, low, largest):
    def one(position, shards_of):
        steps = jax.random.uniform(jax.random.fold_in(jax.random.fold_in(rng, 6), position), (shards_of,), jnp.float32, low / len(cuts), largest / len(cuts))
        return jnp.repeat(jnp.exp(steps), extent[position] // shards_of).reshape((-1,) + (1,) * (len(extent) - position - 1))

    level = one(*cuts[0])
    for cut in cuts[1:]:
        level = level * one(*cut)
    return level


def gaussian(rng, dims, deviation, reach, shards=(), held_as=jnp.bfloat16):
    array = deviation * jax.random.normal(rng, dims, jnp.float32)
    if shards:
        array = array * steps_of(rng, dims, shards, -0.22, 0.18)
    return jnp.clip(array, -reach, reach).astype(held_as)


def setup_inputs(seed: int = 0) -> dict:
    arg_keys = jax.random.split(jax.random.key(seed), 7)
    return {
        "activations": gaussian(arg_keys[0], (TOKENS, D), 1.0, 6.0, ((0, 64), (1, 16))),
        "projection": gaussian(arg_keys[1], (D, RANK), RANK ** -0.5, 0.5),
        "grad_gate": gaussian(arg_keys[2], (TOKENS, FF), (0.125 / (TOK_DEV * N_DP) ** 0.5), 0.0078125, ((0, 64), (1, 16))),
        "grad_up": gaussian(arg_keys[3], (TOKENS, FF), (0.125 / (TOK_DEV * N_DP) ** 0.5), 0.0078125, ((0, 64), (1, 16))),
        "first_moment": gaussian(arg_keys[4], (RANK, 2, FF), 0.1, 0.625, ((0, 64), (2, 16)), jnp.float32),
        "second_moment": jnp.clip(jnp.exp(math.log(0.5) - 2.3025851 * jax.random.uniform(arg_keys[5], (RANK, 2, FF), jnp.float32) ** steps_of(arg_keys[5], (RANK, 2, FF), ((0, 64), (2, 16)), -0.2, 0.2)), 0.05, 0.5),
    }


def reference(activations, projection, grad_gate, grad_up, first_moment, second_moment):
    block_cols = D // N_TENSOR
    act_blocks = activations.reshape(activations.shape[0], N_TENSOR, block_cols).astype(jnp.float32)
    proj_blocks = projection.reshape(N_TENSOR, block_cols, projection.shape[1]).astype(jnp.float32)
    basis_part = jnp.einsum('tjd,jdr->jtr', act_blocks, proj_blocks).astype(jnp.bfloat16)
    token_basis = lax.optimization_barrier(jnp.sum(basis_part.astype(jnp.float32), axis=0)).astype(jnp.bfloat16)
    basis_t = token_basis.T
    gate_low = jnp.dot(basis_t, grad_gate, preferred_element_type=jnp.float32)
    up_low = jnp.dot(basis_t, grad_up, preferred_element_type=jnp.float32)
    grad_low = jnp.stack([gate_low, up_low], axis=1)
    new_first = 0.9 * first_moment + 0.1 * grad_low
    new_second = 0.999 * second_moment + 0.001 * grad_low * grad_low
    corr_one = 1.0 - 0.9 ** STEP
    corr_two = 1.0 - 0.999 ** STEP
    adam_step = new_first / corr_one / (jnp.sqrt(new_second / corr_two) + 1e-08)
    proj_full = projection.astype(jnp.float32)
    gate_update = jnp.dot(proj_full, adam_step[:, 0, :], precision=lax.Precision.HIGHEST).astype(jnp.bfloat16)
    up_update = jnp.dot(proj_full, adam_step[:, 1, :], precision=lax.Precision.HIGHEST).astype(jnp.bfloat16)
    return (gate_update, up_update, new_first, new_second)
```

```python
import dataclasses
import functools

import jax
import jax.numpy as jnp
from jax import lax
from jax.experimental import pallas as pl
from jax.experimental.pallas import tpu as pltpu
from jax.sharding import PartitionSpec as P

STEP = 1000
BF16 = jnp.bfloat16
F32 = jnp.float32
MESH = pl.DeviceIdType.MESH


@dataclasses.dataclass(frozen=True)
class Cfg:
    ny: int
    nzl: int
    tok: int
    feat: int
    ff: int
    chunks: tuple
    nx: int = 4

    @property
    def pieces(self):
        return self.nx * self.ny

    @property
    def rank(self):
        return 4 * self.pieces

    @property
    def half(self):
        return self.ff // 2

    @property
    def lanes(self):
        out, start = [], 0
        for width in self.chunks:
            out.append((start, width))
            start += width
        return out


def row_select(cfg):
    shape = (cfg.pieces, 16, cfg.rank)
    piece = lax.broadcasted_iota(jnp.int32, shape, 0)
    sub = lax.broadcasted_iota(jnp.int32, shape, 1)
    row = lax.broadcasted_iota(jnp.int32, shape, 2)
    ybits = cfg.ny.bit_length() - 1
    px = lax.shift_right_logical(piece, ybits)
    py = piece & (cfg.ny - 1)
    zh = lax.shift_right_logical(sub, 1) & 1
    target = (px * 2 + zh) * (2 * cfg.ny) + py * 2 + (sub & 1)
    return jnp.where(row == target, 1.0, 0.0).astype(BF16).reshape(cfg.pieces * 16, cfg.rank)


def dot(a, b):
    return jnp.dot(a, b, preferred_element_type=F32)


def dot_nt(a, b):
    return lax.dot_general(a, b, (((1,), (1,)), ((), ())), preferred_element_type=F32)


def comm_kernel(cfg, *refs):
    nk = len(cfg.chunks)
    nx, ny, nzl, half = cfg.nx, cfg.ny, cfg.nzl, cfg.half
    nyh, htok, wide = ny // 2, cfg.tok // 2, cfg.pieces * 16
    (act, proj, gg, gu, m1, m2), refs = refs[:6], refs[6:]
    g_outs, refs = refs[:nk], refs[nk:]
    (pw_out, nf_out, ns_out), refs = refs[:3], refs[3:]
    (act_v, pp_v, g_v, pr_v, sel_v, pw_v, w_v, mm, ml, nfl, nsl), refs = refs[:11], refs[11:]
    (part_v, csend, crecv, zsend, zrecv, basis_v), refs = refs[:6], refs[6:]
    names = ("p", "rx1", "sx2", "rx2", "sy", "ry", "sz", "rz", "tf", "g")
    bufs = {}
    for name in names:
        bufs[name], refs = refs[:nk], refs[nk:]
    load_sem, send_sem, recv_sem = refs

    dp, tensor = lax.axis_index("dp"), lax.axis_index("tensor")
    core, zl = tensor % 2, tensor // 2
    y, zh, x = dp % ny, (dp // ny) % 2, dp // (2 * ny)
    xa = x + 1 - 2 * (x % 2)
    xb = (nx - 1) - x
    xo = (x + 2) % nx

    def at_x(other):
        return ((other * 2 + zh) * ny + y, tensor)

    def at_y(d):
        return ((x * 2 + zh) * ny + (y + d) % ny, tensor)

    def at_z(d):
        return (dp, ((zl + d) % nzl) * 2 + core)

    core_peer = (dp, zl * 2 + 1 - core)
    far_peer = ((x * 2 + 1 - zh) * ny + y, tensor)
    partners = [core_peer, far_peer, at_x(xa), at_x(xb)]
    partners += [at_z(d) for d in range(1, nzl)] + [at_y(d) for d in range(1, ny)]

    counts = {"local": 0, "remote": 0}
    remote = []

    def local_copy(src, dst):
        copy = pltpu.make_async_copy(src, dst, load_sem.at[counts["local"]])
        counts["local"] += 1
        copy.start()
        return copy

    def send(src, dst, device):
        index = counts["remote"]
        counts["remote"] += 1
        copy = pltpu.make_async_remote_copy(
            src_ref=src,
            dst_ref=dst,
            send_sem=send_sem.at[index],
            recv_sem=recv_sem.at[index],
            device_id=device,
            device_id_type=MESH,
        )
        copy.start()
        remote.append(copy)
        return copy

    load_act = local_copy(act, act_v)
    load_pp = local_copy(proj.at[pl.ds(pl.multiple_of(tensor * cfg.feat, cfg.feat), cfg.feat)], pp_v)
    barrier = pltpu.get_barrier_semaphore()
    for partner in partners:
        pl.semaphore_signal(barrier, inc=1, device_id=partner, device_id_type=MESH)
    out_rows = pr_v.shape[0]
    load_pr = local_copy(proj.at[pl.ds(pl.multiple_of(dp * out_rows, out_rows), out_rows)], pr_v)
    load_m = [local_copy(m1, mm.at[zh, 0]), local_copy(m2, mm.at[zh, 1])]
    load_g = []
    for q, (ref, h) in enumerate(((gg, 0), (gg, 1), (gu, 0), (gu, 1))):
        load_g.append(local_copy(ref.at[:, pl.ds(h * half, half)], g_v.at[pl.ds(q * cfg.tok, cfg.tok)]))

    load_act.wait()
    load_pp.wait()
    part = dot(act_v[...], pp_v[...])
    part_v[...] = part.reshape(2, htok, cfg.rank)
    csend[...] = part_v[1 - core].astype(BF16)
    sel_v[...] = row_select(cfg)
    for copy in load_m:
        copy.wait()

    pl.semaphore_wait(barrier, len(partners))

    to_core = send(csend, crecv, core_peer)
    moments = send(mm.at[zh], mm.at[zh], far_peer)
    load_pr.wait()
    rows_wide = dot_nt(pr_v[...], sel_v[...])
    lane_quarter = lax.shift_right_logical(lax.broadcasted_iota(jnp.int32, rows_wide.shape, 1), 2) & 3
    for q in range(4):
        pw_v[q] = jnp.where(lane_quarter == q, rows_wide, 0.0).astype(BF16)
    save_pw = local_copy(pw_v, pw_out)
    to_core.wait_recv()
    mine = part_v[core] + crecv[...].astype(F32)
    zsend[...] = mine.astype(BF16)
    part_v[core] = mine
    to_chips = [send(zsend, zrecv.at[d - 1], at_z(d)) for d in range(1, nzl)]
    for copy in load_g:
        copy.wait()
    for copy in to_chips:
        copy.wait_recv()
    total = part_v[core]
    for d in range(1, nzl):
        total = total + zrecv[d - 1].astype(F32)
    basis_v[core] = total.astype(BF16)
    finished = send(basis_v.at[core], basis_v.at[core], core_peer)
    finished.wait_recv()

    basis = basis_v[...].reshape(cfg.tok, cfg.rank)
    basis_wide = dot_nt(sel_v[...], basis)
    sub_quarter = lax.shift_right_logical(lax.broadcasted_iota(jnp.int32, basis_wide.shape, 0), 2) & 3
    for q in range(4):
        w_v[:, q * cfg.tok : (q + 1) * cfg.tok] = jnp.where(sub_quarter == q, basis_wide, 0.0).astype(BF16)

    def block(xblock, colour):
        return pl.ds(xblock * ny + colour * nyh, nyh)

    first = []
    for k, (start, width) in enumerate(cfg.lanes):
        p, rx1 = bufs["p"][k], bufs["rx1"][k]
        grads = g_v[:, start : start + width]
        p[...] = dot(w_v[...], grads).astype(BF16).reshape(cfg.pieces, 16, width)
        first.append(
            [
                send(p.at[block(xa, 0)], rx1.at[0, 0], at_x(xa)),
                send(p.at[block(xb, 1)], rx1.at[1, 0], at_x(xb)),
                send(p.at[block(xo, 0)], rx1.at[0, 1], at_x(xa)),
                send(p.at[block(xo, 1)], rx1.at[1, 1], at_x(xb)),
            ]
        )

    moments.wait_recv()
    for which in range(2):
        for end in range(2):
            for j in range(2):
                for q in range(4):
                    ml[which, pl.ds(4 * q + 2 * end + j, 1), :] = mm[
                        end, which, j, pl.ds(q // 2, 1), pl.ds((q % 2) * half, half)
                    ]

    second = []
    for k in range(nk):
        p, rx1, sx2, rx2 = (bufs[name][k] for name in ("p", "rx1", "sx2", "rx2"))
        for copy in first[k]:
            copy.wait_recv()
        copies = []
        for colour, other in ((0, xb), (1, xa)):
            sx2[colour] = (p[block(other, colour)].astype(F32) + rx1[colour, 1].astype(F32)).astype(BF16)
            copies.append(send(sx2.at[colour], rx2.at[colour], at_x(other)))
        second.append(copies)

    third = []
    for k in range(nk):
        p, rx1, rx2, sy, ry = (bufs[name][k] for name in ("p", "rx1", "rx2", "sy", "ry"))
        for copy in second[k]:
            copy.wait_recv()
        for colour in range(2):
            own = p[block(x, colour)].astype(F32) + rx1[colour, 0].astype(F32) + rx2[colour].astype(F32)
            sy[pl.ds(colour * nyh, nyh)] = own.astype(BF16)
        third.append([send(sy.at[(y + d) % ny], ry.at[d - 1], at_y(d)) for d in range(1, ny)])

    fourth = []
    for k in range(nk):
        sy, ry, sz, rz, tf = (bufs[name][k] for name in ("sy", "ry", "sz", "rz", "tf"))
        for copy in third[k]:
            copy.wait_recv()
        total = sy[y].astype(F32)
        for d in range(1, ny):
            total = total + ry[d - 1].astype(F32)
        tf[...] = total
        sz[...] = total.astype(BF16)
        fourth.append(send(sz, rz, far_peer))

    corr_one = 1.0 - 0.9**STEP
    corr_two = 1.0 - 0.999**STEP
    fifth = []
    for k, (start, width) in enumerate(cfg.lanes):
        rz, tf, g = (bufs[name][k] for name in ("rz", "tf", "g"))
        fourth[k].wait_recv()
        cols = pl.ds(start, width)
        grad = tf[...] + rz[...].astype(F32)
        new_first = 0.9 * ml[0, :, cols] + 0.1 * grad
        new_second = 0.999 * ml[1, :, cols] + 0.001 * grad * grad
        step = new_first / corr_one / (jnp.sqrt(new_second / corr_two) + 1e-08)
        g[x * ny + y] = step.astype(BF16)
        fifth.append([send(g.at[x * ny + y], g.at[x * ny + y], at_y(d)) for d in range(1, ny)])
        nfl[:, cols] = new_first
        nsl[:, cols] = new_second

    sixth = []
    for k in range(nk):
        g = bufs["g"][k]
        for copy in fifth[k]:
            copy.wait_recv()
        copies = []
        for colour, near, far in ((0, xb, xa), (1, xa, xb)):
            copies.append(send(g.at[block(x, colour)], g.at[block(x, colour)], at_x(near)))
        for colour, near, far in ((0, xb, xa), (1, xa, xb)):
            copies.append(send(g.at[block(x, colour)], g.at[block(x, colour)], at_x(far)))
        sixth.append(copies)

    for j in range(2):
        for q in range(4):
            for flat, out in ((nfl, nf_out), (nsl, ns_out)):
                out[j, pl.ds(q // 2, 1), pl.ds((q % 2) * half, half)] = flat[pl.ds(4 * q + j + 2 * zh, 1), :]

    seventh = []
    for k in range(nk):
        g = bufs["g"][k]
        copies = []
        for colour, near, far in ((0, xb, xa), (1, xa, xb)):
            sixth[k][colour].wait_recv()
            copies.append(send(g.at[block(near, colour)], g.at[block(near, colour)], at_x(far)))
        seventh.append(copies)

    saves = []
    for k in range(nk):
        for copy in sixth[k][2:] + seventh[k]:
            copy.wait_recv()
        saves.append(local_copy(bufs["g"][k], g_outs[k]))
    for copy in remote:
        copy.wait_send()
    save_pw.wait()
    for copy in saves:
        copy.wait()


def update_kernel(cfg, *refs):
    nk = len(cfg.chunks)
    gs, refs = refs[:nk], refs[nk:]
    pw, nf, ns, gate, up, nf_out, ns_out, refs = *refs[:7], refs[7:]
    g_vs, refs = refs[:nk], refs[nk:]
    out_vs, refs = refs[:nk], refs[nk:]
    pw_v, sem = refs
    loads = [pltpu.make_async_copy(pw, pw_v, sem.at[0])]
    loads += [pltpu.make_async_copy(gs[k], g_vs[k], sem.at[1 + k]) for k in range(nk)]
    for copy in loads:
        copy.start()
    nf_out[...] = nf[...]
    ns_out[...] = ns[...]
    loads[0].wait()
    saves = []
    for k, (start, width) in enumerate(cfg.lanes):
        loads[1 + k].wait()
        steps = g_vs[k][...].reshape(cfg.pieces * 16, width)
        for q, out in enumerate((gate, gate, up, up)):
            out_vs[k][q] = dot(pw_v[q], steps).astype(BF16)
            columns = pl.ds((q % 2) * cfg.half + start, width)
            copy = pltpu.make_async_copy(out_vs[k].at[q], out.at[:, columns], sem.at[1 + nk + 4 * k + q])
            copy.start()
            saves.append(copy)
    for copy in saves:
        copy.wait()


def shards(cfg, activations, projection, grad_gate, grad_up, first_moment, second_moment):
    nk = len(cfg.chunks)
    out_rows = projection.shape[0] // (2 * cfg.pieces)
    wide, nyh, htok = cfg.pieces * 16, cfg.ny // 2, cfg.tok // 2
    any_spec = pl.BlockSpec(memory_space=pl.ANY)
    vmem_spec = pl.BlockSpec(memory_space=pltpu.VMEM)
    small = jax.ShapeDtypeStruct(first_moment.shape, F32)

    def chunked(*shape, dtype=BF16):
        return [pltpu.VMEM((*shape, width), dtype) for width in cfg.chunks]

    remote_copies = 3 + (cfg.nzl - 1) + nk * (4 + 2 + 2 * (cfg.ny - 1) + 1 + 6)
    scratch = [
        pltpu.VMEM((cfg.tok, cfg.feat), BF16),
        pltpu.VMEM((cfg.feat, cfg.rank), BF16),
        pltpu.VMEM((4 * cfg.tok, cfg.half), BF16),
        pltpu.VMEM((out_rows, cfg.rank), BF16),
        pltpu.VMEM((wide, cfg.rank), BF16),
        pltpu.VMEM((4, out_rows, wide), BF16),
        pltpu.VMEM((wide, 4 * cfg.tok), BF16),
        pltpu.VMEM((2, 2, 2, 2, cfg.ff), F32),
        pltpu.VMEM((2, 16, cfg.half), F32),
        pltpu.VMEM((16, cfg.half), F32),
        pltpu.VMEM((16, cfg.half), F32),
        pltpu.VMEM((2, htok, cfg.rank), F32),
        pltpu.VMEM((htok, cfg.rank), BF16),
        pltpu.VMEM((htok, cfg.rank), BF16),
        pltpu.VMEM((htok, cfg.rank), BF16),
        pltpu.VMEM((cfg.nzl - 1, htok, cfg.rank), BF16),
        pltpu.VMEM((2, htok, cfg.rank), BF16),
        *chunked(cfg.pieces, 16),
        *chunked(2, 2, nyh, 16),
        *chunked(2, nyh, 16),
        *chunked(2, nyh, 16),
        *chunked(cfg.ny, 16),
        *chunked(cfg.ny - 1, 16),
        *chunked(16),
        *chunked(16),
        *chunked(16, dtype=F32),
        *chunked(cfg.pieces, 16),
        pltpu.SemaphoreType.DMA((10 + nk,)),
        pltpu.SemaphoreType.DMA((remote_copies,)),
        pltpu.SemaphoreType.DMA((remote_copies,)),
    ]
    gathered = [jax.ShapeDtypeStruct((cfg.pieces, 16, width), BF16) for width in cfg.chunks]
    *steps, rows_wide, new_first, new_second = pl.pallas_call(
        functools.partial(comm_kernel, cfg),
        out_shape=(*gathered, jax.ShapeDtypeStruct((4, out_rows, wide), BF16), small, small),
        in_specs=[any_spec] * 6,
        out_specs=(*[any_spec] * nk, any_spec, vmem_spec, vmem_spec),
        scratch_shapes=scratch,
        compiler_params=pltpu.CompilerParams(collective_id=0, has_side_effects=True, vmem_limit_bytes=48 << 20),
        name="comm",
    )(activations, projection, grad_gate, grad_up, first_moment, second_moment)
    update = jax.ShapeDtypeStruct((out_rows, cfg.ff), BF16)
    return pl.pallas_call(
        functools.partial(update_kernel, cfg),
        out_shape=(update, update, small, small),
        in_specs=[any_spec] * (nk + 1) + [vmem_spec] * 2,
        out_specs=(any_spec, any_spec, vmem_spec, vmem_spec),
        scratch_shapes=[
            *chunked(cfg.pieces, 16),
            *chunked(4, out_rows),
            pltpu.VMEM((4, out_rows, wide), BF16),
            pltpu.SemaphoreType.DMA((1 + 5 * nk,)),
        ],
        compiler_params=pltpu.CompilerParams(vmem_limit_bytes=48 << 20),
        name="update",
    )(*steps, rows_wide, new_first, new_second)


def build(mesh, cfg):
    in_specs = (
        P("dp", "tensor"),
        P(),
        P("dp", "tensor"),
        P("dp", "tensor"),
        P("dp", None, "tensor"),
        P("dp", None, "tensor"),
    )
    out_specs = (
        P("dp", "tensor"),
        P("dp", "tensor"),
        P("dp", None, "tensor"),
        P("dp", None, "tensor"),
    )
    return jax.shard_map(
        functools.partial(shards, cfg), mesh=mesh, in_specs=in_specs, out_specs=out_specs, check_vma=False
    )


def solution(mesh):
    return build(mesh, Cfg(ny=8, nzl=8, tok=128, feat=512, ff=1792, chunks=(512, 384)))
```

```python
import dataclasses
import functools

import jax
import jax.numpy as jnp
from jax import lax
from jax.experimental import pallas as pl
from jax.experimental.pallas import tpu as pltpu
from jax.sharding import PartitionSpec as P

STEP = 1000
BF16 = jnp.bfloat16
F32 = jnp.float32
MESH = pl.DeviceIdType.MESH


@dataclasses.dataclass(frozen=True)
class Cfg:
    ny: int
    nzl: int
    tok: int
    feat: int
    ff: int
    chunks: tuple
    nx: int = 4

    @property
    def pieces(self):
        return self.nx * self.ny

    @property
    def rank(self):
        return 4 * self.pieces

    @property
    def half(self):
        return self.ff // 2

    @property
    def widths(self):
        return [width for _, _, width in self.chunks]


def row_select(cfg):
    shape = (cfg.pieces, 8, cfg.rank)
    piece = lax.broadcasted_iota(jnp.int32, shape, 0)
    sub = lax.broadcasted_iota(jnp.int32, shape, 1)
    row = lax.broadcasted_iota(jnp.int32, shape, 2)
    ybits = cfg.ny.bit_length() - 1
    px = lax.shift_right_logical(piece, ybits)
    py = piece & (cfg.ny - 1)
    zh = lax.shift_right_logical(sub, 1) & 1
    target = (px * 2 + zh) * (2 * cfg.ny) + py * 2 + (sub & 1)
    return jnp.where(row == target, 1.0, 0.0).astype(BF16).reshape(cfg.pieces * 8, cfg.rank)


def dot(a, b):
    return jnp.dot(a, b, preferred_element_type=F32)


def dot_nt(a, b):
    return lax.dot_general(a, b, (((1,), (1,)), ((), ())), preferred_element_type=F32)


def comm_kernel(cfg, *refs):
    nk = len(cfg.chunks)
    nx, ny, nzl, half = cfg.nx, cfg.ny, cfg.nzl, cfg.half
    nyh, htok = ny // 2, cfg.tok // 2
    (act, proj, gg, gu, m1, m2), refs = refs[:6], refs[6:]
    g_outs, refs = refs[:nk], refs[nk:]
    (pw_out, nf_out, ns_out), refs = refs[:3], refs[3:]
    (act_v, pp_v, g_v, pr_v, sel_v, pw_v, w_v, mm, ml, nfl, nsl), refs = refs[:11], refs[11:]
    (part_v, csend, crecv, zsend, zrecv, basis_v), refs = refs[:6], refs[6:]
    names = ("p", "rx1", "sx2", "rx2", "sy", "ry", "sz", "rz", "tf", "g")
    bufs = {}
    for name in names:
        bufs[name], refs = refs[:nk], refs[nk:]
    load_sem, send_sem, recv_sem = refs

    dp, tensor = lax.axis_index("dp"), lax.axis_index("tensor")
    core, zl = tensor % 2, tensor // 2
    y, zh, x = dp % ny, (dp // ny) % 2, dp // (2 * ny)
    xa = x + 1 - 2 * (x % 2)
    xb = (nx - 1) - x
    xo = (x + 2) % nx

    def at_x(other):
        return ((other * 2 + zh) * ny + y, tensor)

    def at_y(d):
        return ((x * 2 + zh) * ny + (y + d) % ny, tensor)

    def at_z(d):
        return (dp, ((zl + d) % nzl) * 2 + core)

    y_order = sorted(range(1, ny), key=lambda d: -min(d, ny - d))
    z_order = list(range(nzl - 1, 0, -1))
    core_peer = (dp, zl * 2 + 1 - core)
    far_peer = ((x * 2 + 1 - zh) * ny + y, tensor)
    partners = [core_peer, far_peer, at_x(xa), at_x(xb)]
    partners += [at_z(d) for d in range(1, nzl)] + [at_y(d) for d in range(1, ny)]

    counts = {"local": 0, "remote": 0}
    remote = []

    def local_copy(src, dst):
        copy = pltpu.make_async_copy(src, dst, load_sem.at[counts["local"]])
        counts["local"] += 1
        copy.start()
        return copy

    def send(src, dst, device):
        index = counts["remote"]
        counts["remote"] += 1
        copy = pltpu.make_async_remote_copy(
            src_ref=src,
            dst_ref=dst,
            send_sem=send_sem.at[index],
            recv_sem=recv_sem.at[index],
            device_id=device,
            device_id_type=MESH,
        )
        copy.start()
        remote.append(copy)
        return copy

    load_act = local_copy(act, act_v)
    load_pp = local_copy(proj.at[pl.ds(pl.multiple_of(tensor * cfg.feat, cfg.feat), cfg.feat)], pp_v)
    barrier = pltpu.get_barrier_semaphore()
    for partner in partners:
        pl.semaphore_signal(barrier, inc=1, device_id=partner, device_id_type=MESH)
    out_rows = pr_v.shape[0]
    load_pr = local_copy(proj.at[pl.ds(pl.multiple_of(dp * out_rows, out_rows), out_rows)], pr_v)
    load_m = [local_copy(m1, mm.at[zh, 0]), local_copy(m2, mm.at[zh, 1])]
    load_g = []
    for which, ref in enumerate((gg, gu)):
        for h in range(2):
            load_g.append(
                local_copy(ref.at[:, pl.ds(h * half, half)], g_v.at[which, pl.ds(h * cfg.tok, cfg.tok)])
            )

    load_act.wait()
    load_pp.wait()
    part = dot(act_v[...], pp_v[...])
    part_v[...] = part.reshape(2, htok, cfg.rank)
    csend[...] = part_v[1 - core].astype(BF16)
    sel_v[...] = row_select(cfg)
    for copy in load_m:
        copy.wait()

    pl.semaphore_wait(barrier, len(partners))

    to_core = send(csend, crecv, core_peer)
    load_pr.wait()
    rows_wide = dot_nt(pr_v[...], sel_v[...])
    lane_half = lax.shift_right_logical(lax.broadcasted_iota(jnp.int32, rows_wide.shape, 1), 2) & 1
    for h in range(2):
        pw_v[h] = jnp.where(lane_half == h, rows_wide, 0.0).astype(BF16)
    save_pw = local_copy(pw_v, pw_out)
    to_core.wait_recv()
    mine = part_v[core] + crecv[...].astype(F32)
    zsend[...] = mine.astype(BF16)
    part_v[core] = mine
    to_chips = [send(zsend, zrecv.at[d - 1], at_z(d)) for d in z_order]
    for copy in load_g:
        copy.wait()
    for copy in to_chips:
        copy.wait_recv()
    total = part_v[core]
    for d in range(1, nzl):
        total = total + zrecv[d - 1].astype(F32)
    basis_v[core] = total.astype(BF16)
    finished = send(basis_v.at[core], basis_v.at[core], core_peer)
    finished.wait_recv()

    basis = basis_v[...].reshape(cfg.tok, cfg.rank)
    basis_wide = dot_nt(sel_v[...], basis)
    sub_half = lax.shift_right_logical(lax.broadcasted_iota(jnp.int32, basis_wide.shape, 0), 2) & 1
    for h in range(2):
        w_v[:, h * cfg.tok : (h + 1) * cfg.tok] = jnp.where(sub_half == h, basis_wide, 0.0).astype(BF16)

    def block(xblock, colour):
        return pl.ds(xblock * ny + colour * nyh, nyh)

    first = []
    for k, (which, start, width) in enumerate(cfg.chunks):
        p, rx1 = bufs["p"][k], bufs["rx1"][k]
        grads = g_v[which, :, start : start + width]
        p[...] = dot(w_v[...], grads).astype(BF16).reshape(cfg.pieces, 8, width)
        first.append(
            [
                send(p.at[block(xa, 0)], rx1.at[0, 0], at_x(xa)),
                send(p.at[block(xb, 1)], rx1.at[1, 0], at_x(xb)),
                send(p.at[block(xo, 0)], rx1.at[0, 1], at_x(xa)),
                send(p.at[block(xo, 1)], rx1.at[1, 1], at_x(xb)),
            ]
        )

    moments = send(mm.at[zh], mm.at[zh], far_peer)

    second = []
    for k in range(nk):
        p, rx1, sx2, rx2 = (bufs[name][k] for name in ("p", "rx1", "sx2", "rx2"))
        for copy in first[k]:
            copy.wait_recv()
        copies = []
        for colour, other in ((0, xb), (1, xa)):
            sx2[colour] = (p[block(other, colour)].astype(F32) + rx1[colour, 1].astype(F32)).astype(BF16)
            copies.append(send(sx2.at[colour], rx2.at[colour], at_x(other)))
        second.append(copies)

    third = []
    for k in range(nk):
        p, rx1, rx2, sy, ry = (bufs[name][k] for name in ("p", "rx1", "rx2", "sy", "ry"))
        for copy in second[k]:
            copy.wait_recv()
        for colour in range(2):
            own = p[block(x, colour)].astype(F32) + rx1[colour, 0].astype(F32) + rx2[colour].astype(F32)
            sy[pl.ds(colour * nyh, nyh)] = own.astype(BF16)
        third.append([send(sy.at[(y + d) % ny], ry.at[d - 1], at_y(d)) for d in y_order])

    moments.wait_recv()
    for moment in range(2):
        for end in range(2):
            for j in range(2):
                for which in range(2):
                    for h in range(2):
                        ml[moment, pl.ds(4 * h + 2 * end + j, 1), pl.ds(which * half, half)] = mm[
                            end, moment, j, pl.ds(which, 1), pl.ds(h * half, half)
                        ]

    fourth = []
    for k in range(nk):
        sy, ry, sz, rz, tf = (bufs[name][k] for name in ("sy", "ry", "sz", "rz", "tf"))
        for copy in third[k]:
            copy.wait_recv()
        total = sy[y].astype(F32)
        for d in range(1, ny):
            total = total + ry[d - 1].astype(F32)
        tf[...] = total
        sz[...] = total.astype(BF16)
        fourth.append(send(sz, rz, far_peer))

    corr_one = 1.0 - 0.9**STEP
    corr_two = 1.0 - 0.999**STEP
    fifth = []
    for k, (which, start, width) in enumerate(cfg.chunks):
        rz, tf, g = (bufs[name][k] for name in ("rz", "tf", "g"))
        fourth[k].wait_recv()
        cols = pl.ds(which * half + start, width)
        grad = tf[...] + rz[...].astype(F32)
        new_first = 0.9 * ml[0, :, cols] + 0.1 * grad
        new_second = 0.999 * ml[1, :, cols] + 0.001 * grad * grad
        step = new_first / corr_one / (jnp.sqrt(new_second / corr_two) + 1e-08)
        g[x * ny + y] = step.astype(BF16)
        fifth.append([send(g.at[x * ny + y], g.at[x * ny + y], at_y(d)) for d in y_order])
        nfl[:, cols] = new_first
        nsl[:, cols] = new_second

    sixth = []
    for k in range(nk):
        g = bufs["g"][k]
        for copy in fifth[k]:
            copy.wait_recv()
        copies = []
        for colour, near, far in ((0, xb, xa), (1, xa, xb)):
            copies.append(send(g.at[block(x, colour)], g.at[block(x, colour)], at_x(near)))
        for colour, near, far in ((0, xb, xa), (1, xa, xb)):
            copies.append(send(g.at[block(x, colour)], g.at[block(x, colour)], at_x(far)))
        sixth.append(copies)

    for j in range(2):
        for which in range(2):
            for h in range(2):
                for flat, out in ((nfl, nf_out), (nsl, ns_out)):
                    out[j, pl.ds(which, 1), pl.ds(h * half, half)] = flat[
                        pl.ds(4 * h + j + 2 * zh, 1), pl.ds(which * half, half)
                    ]

    seventh = []
    for k in range(nk):
        g = bufs["g"][k]
        copies = []
        for colour, near, far in ((0, xb, xa), (1, xa, xb)):
            sixth[k][colour].wait_recv()
            copies.append(send(g.at[block(near, colour)], g.at[block(near, colour)], at_x(far)))
        seventh.append(copies)

    saves = []
    for k in range(nk):
        for copy in sixth[k][2:] + seventh[k]:
            copy.wait_recv()
        saves.append(local_copy(bufs["g"][k], g_outs[k]))
    for copy in remote:
        copy.wait_send()
    save_pw.wait()
    for copy in saves:
        copy.wait()


def update_kernel(cfg, *refs):
    nk = len(cfg.chunks)
    gs, refs = refs[:nk], refs[nk:]
    pw, nf, ns, gate, up, nf_out, ns_out, refs = *refs[:7], refs[7:]
    g_vs, refs = refs[:nk], refs[nk:]
    out_vs, refs = refs[:nk], refs[nk:]
    pw_v, sem = refs
    loads = [pltpu.make_async_copy(pw, pw_v, sem.at[0])]
    loads += [pltpu.make_async_copy(gs[k], g_vs[k], sem.at[1 + k]) for k in range(nk)]
    for copy in loads:
        copy.start()
    nf_out[...] = nf[...]
    ns_out[...] = ns[...]
    loads[0].wait()
    saves = []
    for k, (which, start, width) in enumerate(cfg.chunks):
        loads[1 + k].wait()
        steps = g_vs[k][...].reshape(cfg.pieces * 8, width)
        for h in range(2):
            out_vs[k][h] = dot(pw_v[h], steps).astype(BF16)
            columns = pl.ds(h * cfg.half + start, width)
            copy = pltpu.make_async_copy(
                out_vs[k].at[h], (gate, up)[which].at[:, columns], sem.at[1 + nk + 2 * k + h]
            )
            copy.start()
            saves.append(copy)
    for copy in saves:
        copy.wait()


def shards(cfg, activations, projection, grad_gate, grad_up, first_moment, second_moment):
    nk = len(cfg.chunks)
    out_rows = projection.shape[0] // (2 * cfg.pieces)
    wide, nyh, htok = cfg.pieces * 8, cfg.ny // 2, cfg.tok // 2
    any_spec = pl.BlockSpec(memory_space=pl.ANY)
    vmem_spec = pl.BlockSpec(memory_space=pltpu.VMEM)
    small = jax.ShapeDtypeStruct(first_moment.shape, F32)

    def chunked(*shape, dtype=BF16):
        return [pltpu.VMEM((*shape, width), dtype) for width in cfg.widths]

    remote_copies = 3 + (cfg.nzl - 1) + nk * (4 + 2 + 2 * (cfg.ny - 1) + 1 + 6)
    scratch = [
        pltpu.VMEM((cfg.tok, cfg.feat), BF16),
        pltpu.VMEM((cfg.feat, cfg.rank), BF16),
        pltpu.VMEM((2, 2 * cfg.tok, cfg.half), BF16),
        pltpu.VMEM((out_rows, cfg.rank), BF16),
        pltpu.VMEM((wide, cfg.rank), BF16),
        pltpu.VMEM((2, out_rows, wide), BF16),
        pltpu.VMEM((wide, 2 * cfg.tok), BF16),
        pltpu.VMEM((2, 2, 2, 2, cfg.ff), F32),
        pltpu.VMEM((2, 8, cfg.ff), F32),
        pltpu.VMEM((8, cfg.ff), F32),
        pltpu.VMEM((8, cfg.ff), F32),
        pltpu.VMEM((2, htok, cfg.rank), F32),
        pltpu.VMEM((htok, cfg.rank), BF16),
        pltpu.VMEM((htok, cfg.rank), BF16),
        pltpu.VMEM((htok, cfg.rank), BF16),
        pltpu.VMEM((cfg.nzl - 1, htok, cfg.rank), BF16),
        pltpu.VMEM((2, htok, cfg.rank), BF16),
        *chunked(cfg.pieces, 8),
        *chunked(2, 2, nyh, 8),
        *chunked(2, nyh, 8),
        *chunked(2, nyh, 8),
        *chunked(cfg.ny, 8),
        *chunked(cfg.ny - 1, 8),
        *chunked(8),
        *chunked(8),
        *chunked(8, dtype=F32),
        *chunked(cfg.pieces, 8),
        pltpu.SemaphoreType.DMA((10 + nk,)),
        pltpu.SemaphoreType.DMA((remote_copies,)),
        pltpu.SemaphoreType.DMA((remote_copies,)),
    ]
    gathered = [jax.ShapeDtypeStruct((cfg.pieces, 8, width), BF16) for width in cfg.widths]
    *steps, rows_wide, new_first, new_second = pl.pallas_call(
        functools.partial(comm_kernel, cfg),
        out_shape=(*gathered, jax.ShapeDtypeStruct((2, out_rows, wide), BF16), small, small),
        in_specs=[pl.BlockSpec(memory_space=pltpu.HBM)] * 6,
        out_specs=(*[any_spec] * nk, any_spec, vmem_spec, vmem_spec),
        scratch_shapes=scratch,
        compiler_params=pltpu.CompilerParams(collective_id=0, has_side_effects=True, vmem_limit_bytes=67043328),
        name="comm",
    )(activations, projection, grad_gate, grad_up, first_moment, second_moment)
    update = jax.ShapeDtypeStruct((out_rows, cfg.ff), BF16)
    return pl.pallas_call(
        functools.partial(update_kernel, cfg),
        out_shape=(update, update, small, small),
        in_specs=[any_spec] * (nk + 1) + [vmem_spec] * 2,
        out_specs=(any_spec, any_spec, vmem_spec, vmem_spec),
        scratch_shapes=[
            *chunked(cfg.pieces, 8),
            *chunked(2, out_rows),
            pltpu.VMEM((2, out_rows, wide), BF16),
            pltpu.SemaphoreType.DMA((1 + 3 * nk,)),
        ],
        compiler_params=pltpu.CompilerParams(vmem_limit_bytes=67043328),
        name="update",
    )(*steps, rows_wide, new_first, new_second)


def build(mesh, cfg):
    in_specs = (
        P("dp", "tensor"),
        P(),
        P("dp", "tensor"),
        P("dp", "tensor"),
        P("dp", None, "tensor"),
        P("dp", None, "tensor"),
    )
    out_specs = (
        P("dp", "tensor"),
        P("dp", "tensor"),
        P("dp", None, "tensor"),
        P("dp", None, "tensor"),
    )
    return jax.shard_map(
        functools.partial(shards, cfg), mesh=mesh, in_specs=in_specs, out_specs=out_specs, check_vma=False
    )


def solution(mesh):
    return build(mesh, Cfg(ny=8, nzl=8, tok=128, feat=512, ff=1792, chunks=((0, 0, 896), (1, 0, 896))))
```

```python
import dataclasses
import functools

import jax
import jax.numpy as jnp
from jax import lax
from jax.experimental import pallas as pl
from jax.experimental.pallas import tpu as pltpu
from jax.sharding import PartitionSpec as P

STEP = 1000
BF16 = jnp.bfloat16
F32 = jnp.float32
MESH = pl.DeviceIdType.MESH


@dataclasses.dataclass(frozen=True)
class Cfg:
    ny: int
    nzl: int
    tok: int
    feat: int
    ff: int
    chunks: tuple
    nx: int = 4

    @property
    def pieces(self):
        return self.nx * self.ny

    @property
    def rank(self):
        return 4 * self.pieces

    @property
    def half(self):
        return self.ff // 2

    @property
    def widths(self):
        return [width for _, _, width in self.chunks]


def row_select(cfg):
    shape = (cfg.pieces, 8, cfg.rank)
    piece = lax.broadcasted_iota(jnp.int32, shape, 0)
    sub = lax.broadcasted_iota(jnp.int32, shape, 1)
    row = lax.broadcasted_iota(jnp.int32, shape, 2)
    ybits = cfg.ny.bit_length() - 1
    px = lax.shift_right_logical(piece, ybits)
    py = piece & (cfg.ny - 1)
    zh = lax.shift_right_logical(sub, 1) & 1
    target = (px * 2 + zh) * (2 * cfg.ny) + py * 2 + (sub & 1)
    return jnp.where(row == target, 1.0, 0.0).astype(BF16).reshape(cfg.pieces * 8, cfg.rank)


def dot(a, b):
    return jnp.dot(a, b, preferred_element_type=F32)


def dot_nt(a, b):
    return lax.dot_general(a, b, (((1,), (1,)), ((), ())), preferred_element_type=F32)


def comm_kernel(cfg, *refs):
    nk = len(cfg.chunks)
    nx, ny, nzl, half = cfg.nx, cfg.ny, cfg.nzl, cfg.half
    nyh, zhalf, htok = ny // 2, nzl // 2, cfg.tok // 2
    (act, proj, gg, gu, m1, m2), refs = refs[:6], refs[6:]
    g_outs, refs = refs[:nk], refs[nk:]
    (pw_out, nf_out, ns_out), refs = refs[:3], refs[3:]
    (act_v, pp_v, g_v, pr_v, sel_v, pw_v, w_v, mm, ml, nfl, nsl), refs = refs[:11], refs[11:]
    (part_v, csend, crecv, zsend, zpair, zrecv, basis_v), refs = refs[:7], refs[7:]
    names = ("p", "rx1", "sx2", "rx2", "sy", "ry", "sz", "rz", "tf")
    bufs = {"g": g_outs}
    for name in names:
        bufs[name], refs = refs[:nk], refs[nk:]
    load_sem, send_sem, recv_sem = refs

    dp, tensor = lax.axis_index("dp"), lax.axis_index("tensor")
    core, zl = tensor % 2, tensor // 2
    y, zh, x = dp % ny, (dp // ny) % 2, dp // (2 * ny)
    xa = x + 1 - 2 * (x % 2)
    xb = (nx - 1) - x
    xo = (x + 2) % nx

    def at_x(other):
        return ((other * 2 + zh) * ny + y, tensor)

    def at_y(d):
        return ((x * 2 + zh) * ny + (y + d) % ny, tensor)

    def at_z(d):
        return (dp, ((zl + d) % nzl) * 2 + core)

    y_order = sorted(range(1, ny), key=lambda d: -min(d, ny - d))
    def at_z_half(d):
        return (dp, ((zl // zhalf) * zhalf + (zl + d) % zhalf) * 2 + core)

    core_peer = (dp, zl * 2 + 1 - core)
    far_peer = ((x * 2 + 1 - zh) * ny + y, tensor)
    partners = [core_peer, far_peer, at_x(xa), at_x(xb)]
    partners += [at_z(zhalf)] + [at_z_half(d) for d in range(1, zhalf)] + [at_y(d) for d in range(1, ny)]

    counts = {"local": 0, "remote": 0}
    remote = []

    def local_copy(src, dst):
        copy = pltpu.make_async_copy(src, dst, load_sem.at[counts["local"]])
        counts["local"] += 1
        copy.start()
        return copy

    def send(src, dst, device):
        index = counts["remote"]
        counts["remote"] += 1
        copy = pltpu.make_async_remote_copy(
            src_ref=src,
            dst_ref=dst,
            send_sem=send_sem.at[index],
            recv_sem=recv_sem.at[index],
            device_id=device,
            device_id_type=MESH,
        )
        copy.start()
        remote.append(copy)
        return copy

    load_act = local_copy(act, act_v)
    load_pp = local_copy(proj.at[pl.ds(pl.multiple_of(tensor * cfg.feat, cfg.feat), cfg.feat)], pp_v)
    barrier = pltpu.get_barrier_semaphore()
    for partner in partners:
        pl.semaphore_signal(barrier, inc=1, device_id=partner, device_id_type=MESH)
    out_rows = pr_v.shape[0]
    load_pr = local_copy(proj.at[pl.ds(pl.multiple_of(dp * out_rows, out_rows), out_rows)], pr_v)
    load_m = [local_copy(m1, mm.at[zh, 0]), local_copy(m2, mm.at[zh, 1])]
    load_g = []
    for which, ref in enumerate((gg, gu)):
        for h in range(2):
            load_g.append(
                local_copy(ref.at[:, pl.ds(h * half, half)], g_v.at[which, pl.ds(h * cfg.tok, cfg.tok)])
            )

    load_act.wait()
    load_pp.wait()
    part = dot(act_v[...], pp_v[...])
    part_v[...] = part.reshape(2, htok, cfg.rank)
    csend[...] = part_v[1 - core].astype(BF16)
    sel_v[...] = row_select(cfg)
    for copy in load_m:
        copy.wait()

    pl.semaphore_wait(barrier, len(partners))

    to_core = send(csend, crecv, core_peer)
    load_pr.wait()
    rows_wide = dot_nt(pr_v[...], sel_v[...])
    lane_half = lax.shift_right_logical(lax.broadcasted_iota(jnp.int32, rows_wide.shape, 1), 2) & 1
    for h in range(2):
        pw_v[h] = jnp.where(lane_half == h, rows_wide, 0.0).astype(BF16)
    save_pw = local_copy(pw_v, pw_out)
    to_core.wait_recv()
    mine = part_v[core] + crecv[...].astype(F32)
    zsend[...] = mine.astype(BF16)
    part_v[core] = mine
    across = send(zsend, zrecv.at[0], at_z(zhalf))
    for copy in load_g:
        copy.wait()
    across.wait_recv()
    pair = part_v[core] + zrecv[0].astype(F32)
    zpair[...] = pair.astype(BF16)
    part_v[core] = pair
    to_chips = [send(zpair, zrecv.at[d], at_z_half(d)) for d in range(zhalf - 1, 0, -1)]
    for copy in to_chips:
        copy.wait_recv()
    total = part_v[core]
    for d in range(1, zhalf):
        total = total + zrecv[d].astype(F32)
    basis_v[core] = total.astype(BF16)
    finished = send(basis_v.at[core], basis_v.at[core], core_peer)
    finished.wait_recv()

    basis = basis_v[...].reshape(cfg.tok, cfg.rank)
    basis_wide = dot_nt(sel_v[...], basis)
    sub_half = lax.shift_right_logical(lax.broadcasted_iota(jnp.int32, basis_wide.shape, 0), 2) & 1
    for h in range(2):
        w_v[:, h * cfg.tok : (h + 1) * cfg.tok] = jnp.where(sub_half == h, basis_wide, 0.0).astype(BF16)

    def block(xblock, colour):
        return pl.ds(xblock * ny + colour * nyh, nyh)

    first = []
    for k, (which, start, width) in enumerate(cfg.chunks):
        p, rx1 = bufs["p"][k], bufs["rx1"][k]
        grads = g_v[which, :, start : start + width]
        p[...] = dot(w_v[...], grads).astype(BF16).reshape(cfg.pieces, 8, width)
        first.append(
            [
                send(p.at[block(xa, 0)], rx1.at[0, 0], at_x(xa)),
                send(p.at[block(xb, 1)], rx1.at[1, 0], at_x(xb)),
                send(p.at[block(xo, 0)], rx1.at[0, 1], at_x(xa)),
                send(p.at[block(xo, 1)], rx1.at[1, 1], at_x(xb)),
            ]
        )

    moments = send(mm.at[zh], mm.at[zh], far_peer)

    second = []
    for k in range(nk):
        p, rx1, sx2, rx2 = (bufs[name][k] for name in ("p", "rx1", "sx2", "rx2"))
        for copy in first[k]:
            copy.wait_recv()
        copies = []
        for colour, other in ((0, xb), (1, xa)):
            sx2[colour] = (p[block(other, colour)].astype(F32) + rx1[colour, 1].astype(F32)).astype(BF16)
            copies.append(send(sx2.at[colour], rx2.at[colour], at_x(other)))
        second.append(copies)

    third = []
    for k in range(nk):
        p, rx1, rx2, sy, ry = (bufs[name][k] for name in ("p", "rx1", "rx2", "sy", "ry"))
        for copy in second[k]:
            copy.wait_recv()
        for colour in range(2):
            own = p[block(x, colour)].astype(F32) + rx1[colour, 0].astype(F32) + rx2[colour].astype(F32)
            sy[pl.ds(colour * nyh, nyh)] = own.astype(BF16)
        third.append([send(sy.at[(y + d) % ny], ry.at[d - 1], at_y(d)) for d in y_order])

    moments.wait_recv()
    for moment in range(2):
        for end in range(2):
            for j in range(2):
                for which in range(2):
                    for h in range(2):
                        ml[moment, pl.ds(4 * h + 2 * end + j, 1), pl.ds(which * half, half)] = mm[
                            end, moment, j, pl.ds(which, 1), pl.ds(h * half, half)
                        ]

    fourth = []
    for k in range(nk):
        sy, ry, sz, rz, tf = (bufs[name][k] for name in ("sy", "ry", "sz", "rz", "tf"))
        for copy in third[k]:
            copy.wait_recv()
        total = sy[y].astype(F32)
        for d in range(1, ny):
            total = total + ry[d - 1].astype(F32)
        tf[...] = total
        sz[...] = total.astype(BF16)
        fourth.append(send(sz, rz, far_peer))

    corr_one = 1.0 - 0.9**STEP
    corr_two = 1.0 - 0.999**STEP
    fifth = []
    for k, (which, start, width) in enumerate(cfg.chunks):
        rz, tf, g = (bufs[name][k] for name in ("rz", "tf", "g"))
        fourth[k].wait_recv()
        cols = pl.ds(which * half + start, width)
        grad = tf[...] + rz[...].astype(F32)
        new_first = 0.9 * ml[0, :, cols] + 0.1 * grad
        new_second = 0.999 * ml[1, :, cols] + 0.001 * grad * grad
        step = new_first / corr_one / (jnp.sqrt(new_second / corr_two) + 1e-08)
        g[x * ny + y] = step.astype(BF16)
        fifth.append([send(g.at[x * ny + y], g.at[x * ny + y], at_y(d)) for d in y_order])
        nfl[:, cols] = new_first
        nsl[:, cols] = new_second

    sixth = []
    for k in range(nk):
        g = bufs["g"][k]
        for copy in fifth[k]:
            copy.wait_recv()
        copies = []
        for colour, near, far in ((0, xb, xa), (1, xa, xb)):
            copies.append(send(g.at[block(x, colour)], g.at[block(x, colour)], at_x(near)))
        for colour, near, far in ((0, xb, xa), (1, xa, xb)):
            copies.append(send(g.at[block(x, colour)], g.at[block(x, colour)], at_x(far)))
        sixth.append(copies)

    for j in range(2):
        for which in range(2):
            for h in range(2):
                for flat, out in ((nfl, nf_out), (nsl, ns_out)):
                    out[j, pl.ds(which, 1), pl.ds(h * half, half)] = flat[
                        pl.ds(4 * h + j + 2 * zh, 1), pl.ds(which * half, half)
                    ]

    seventh = []
    for k in range(nk):
        g = bufs["g"][k]
        copies = []
        for colour, near, far in ((0, xb, xa), (1, xa, xb)):
            sixth[k][colour].wait_recv()
            copies.append(send(g.at[block(near, colour)], g.at[block(near, colour)], at_x(far)))
        seventh.append(copies)

    for k in range(nk):
        for copy in sixth[k][2:] + seventh[k]:
            copy.wait_recv()
    for copy in remote:
        copy.wait_send()
    save_pw.wait()


def update_kernel(cfg, *refs):
    nk = len(cfg.chunks)
    gs, refs = refs[:nk], refs[nk:]
    pw, nf, ns, gate, up, nf_out, ns_out, refs = *refs[:7], refs[7:]
    out_vs, (sem,) = refs[:nk], refs[nk:]
    saves = []
    for k, (which, start, width) in enumerate(cfg.chunks):
        steps = gs[k][...].reshape(cfg.pieces * 8, width)
        for h in range(2):
            out_vs[k][h] = dot(pw[h], steps).astype(BF16)
            columns = pl.ds(h * cfg.half + start, width)
            copy = pltpu.make_async_copy(
                out_vs[k].at[h], (gate, up)[which].at[:, columns], sem.at[2 * k + h]
            )
            copy.start()
            saves.append(copy)
    nf_out[...] = nf[...]
    ns_out[...] = ns[...]
    for copy in saves:
        copy.wait()


def shards(cfg, *inputs):
    _, projection, _, _, first_moment, _ = inputs
    nk = len(cfg.chunks)
    out_rows = projection.shape[0] // (2 * cfg.pieces)
    wide, nyh, htok = cfg.pieces * 8, cfg.ny // 2, cfg.tok // 2
    any_spec = pl.BlockSpec(memory_space=pl.ANY)
    vmem_spec = pl.BlockSpec(memory_space=pltpu.VMEM)
    small = jax.ShapeDtypeStruct(first_moment.shape, F32)

    def chunked(*shape, dtype=BF16):
        return [pltpu.VMEM((*shape, width), dtype) for width in cfg.widths]

    remote_copies = 3 + cfg.nzl // 2 + nk * (4 + 2 + 2 * (cfg.ny - 1) + 1 + 6)
    scratch = [
        pltpu.VMEM((cfg.tok, cfg.feat), BF16),
        pltpu.VMEM((cfg.feat, cfg.rank), BF16),
        pltpu.VMEM((2, 2 * cfg.tok, cfg.half), BF16),
        pltpu.VMEM((out_rows, cfg.rank), BF16),
        pltpu.VMEM((wide, cfg.rank), BF16),
        pltpu.VMEM((2, out_rows, wide), BF16),
        pltpu.VMEM((wide, 2 * cfg.tok), BF16),
        pltpu.VMEM((2, 2, 2, 2, cfg.ff), F32),
        pltpu.VMEM((2, 8, cfg.ff), F32),
        pltpu.VMEM((8, cfg.ff), F32),
        pltpu.VMEM((8, cfg.ff), F32),
        pltpu.VMEM((2, htok, cfg.rank), F32),
        pltpu.VMEM((htok, cfg.rank), BF16),
        pltpu.VMEM((htok, cfg.rank), BF16),
        pltpu.VMEM((htok, cfg.rank), BF16),
        pltpu.VMEM((htok, cfg.rank), BF16),
        pltpu.VMEM((cfg.nzl // 2, htok, cfg.rank), BF16),
        pltpu.VMEM((2, htok, cfg.rank), BF16),
        *chunked(cfg.pieces, 8),
        *chunked(2, 2, nyh, 8),
        *chunked(2, nyh, 8),
        *chunked(2, nyh, 8),
        *chunked(cfg.ny, 8),
        *chunked(cfg.ny - 1, 8),
        *chunked(8),
        *chunked(8),
        *chunked(8, dtype=F32),
        pltpu.SemaphoreType.DMA((10,)),
        pltpu.SemaphoreType.DMA((remote_copies,)),
        pltpu.SemaphoreType.DMA((remote_copies,)),
    ]
    gathered = chunked(cfg.pieces, 8)
    *steps, rows_wide, new_first, new_second = pl.pallas_call(
        functools.partial(comm_kernel, cfg),
        out_shape=(*gathered, jax.ShapeDtypeStruct((2, out_rows, wide), BF16), small, small),
        in_specs=[pl.BlockSpec(memory_space=pltpu.HBM)] * 6,
        out_specs=(*[vmem_spec] * nk, any_spec, vmem_spec, vmem_spec),
        scratch_shapes=scratch,
        compiler_params=pltpu.CompilerParams(collective_id=0, has_side_effects=True, vmem_limit_bytes=48 << 20),
        name="comm",
    )(*[pltpu.with_memory_space_constraint(ref, pltpu.HBM) for ref in inputs])
    update = jax.ShapeDtypeStruct((out_rows, cfg.ff), BF16)
    return pl.pallas_call(
        functools.partial(update_kernel, cfg),
        out_shape=(update, update, small, small),
        in_specs=[vmem_spec] * (nk + 3),
        out_specs=(any_spec, any_spec, vmem_spec, vmem_spec),
        scratch_shapes=[
            *chunked(2, out_rows),
            pltpu.SemaphoreType.DMA((2 * nk,)),
        ],
        compiler_params=pltpu.CompilerParams(vmem_limit_bytes=48 << 20),
        name="update",
    )(*steps, rows_wide, new_first, new_second)


def build(mesh, cfg):
    in_specs = (
        P("dp", "tensor"),
        P(),
        P("dp", "tensor"),
        P("dp", "tensor"),
        P("dp", None, "tensor"),
        P("dp", None, "tensor"),
    )
    out_specs = (
        P("dp", "tensor"),
        P("dp", "tensor"),
        P("dp", None, "tensor"),
        P("dp", None, "tensor"),
    )
    return jax.shard_map(
        functools.partial(shards, cfg), mesh=mesh, in_specs=in_specs, out_specs=out_specs, check_vma=False
    )


def solution(mesh):
    return build(mesh, Cfg(ny=8, nzl=8, tok=128, feat=512, ff=1792, chunks=((0, 0, 512), (0, 512, 384), (1, 0, 512), (1, 512, 384))))
```

```python
import dataclasses
import functools

import jax
import jax.numpy as jnp
from jax import lax
from jax.experimental import pallas as pl
from jax.experimental.pallas import tpu as pltpu
from jax.sharding import PartitionSpec as P

STEP = 1000
BF16 = jnp.bfloat16
F32 = jnp.float32
MESH = pl.DeviceIdType.MESH


@dataclasses.dataclass(frozen=True)
class Cfg:
    ny: int
    nzl: int
    tok: int
    feat: int
    ff: int
    chunks: tuple
    nx: int = 4

    @property
    def pieces(self):
        return self.nx * self.ny

    @property
    def rank(self):
        return 4 * self.pieces

    @property
    def half(self):
        return self.ff // 2

    @property
    def widths(self):
        return [width for _, _, width in self.chunks]


def row_select(cfg):
    shape = (cfg.pieces, 8, cfg.rank)
    piece = lax.broadcasted_iota(jnp.int32, shape, 0)
    sub = lax.broadcasted_iota(jnp.int32, shape, 1)
    row = lax.broadcasted_iota(jnp.int32, shape, 2)
    ybits = cfg.ny.bit_length() - 1
    px = lax.shift_right_logical(piece, ybits)
    py = piece & (cfg.ny - 1)
    zh = lax.shift_right_logical(sub, 1) & 1
    target = (px * 2 + zh) * (2 * cfg.ny) + py * 2 + (sub & 1)
    return jnp.where(row == target, 1.0, 0.0).astype(BF16).reshape(cfg.pieces * 8, cfg.rank)


def dot(a, b):
    return jnp.dot(a, b, preferred_element_type=F32)


def dot_nt(a, b):
    return lax.dot_general(a, b, (((1,), (1,)), ((), ())), preferred_element_type=F32)


def comm_kernel(cfg, *refs):
    nk = len(cfg.chunks)
    nx, ny, nzl, half = cfg.nx, cfg.ny, cfg.nzl, cfg.half
    zhalf, htok = nzl // 2, cfg.tok // 2
    (act, proj, gg, gu, m1, m2), refs = refs[:6], refs[6:]
    g_outs, refs = refs[:nk], refs[nk:]
    (pw_out, nf_out, ns_out), refs = refs[:3], refs[3:]
    (act_v, pp_v, g_v, pr_v, sel_v, pw_v, w_v, mm, ml, nfl, nsl), refs = refs[:11], refs[11:]
    (part_v, csend, crecv, zsend, zpair, zrecv, basis_v), refs = refs[:7], refs[7:]
    names = ("p", "rx", "sy", "ry", "sz", "rz", "tf")
    bufs = {"g": g_outs}
    for name in names:
        bufs[name], refs = refs[:nk], refs[nk:]
    load_sem, send_sem, recv_sem = refs

    dp, tensor = lax.axis_index("dp"), lax.axis_index("tensor")
    core, zl = tensor % 2, tensor // 2
    y, zh, x = dp % ny, (dp // ny) % 2, dp // (2 * ny)

    def at_x(other):
        return ((other * 2 + zh) * ny + y, tensor)

    def at_y(d):
        return ((x * 2 + zh) * ny + (y + d) % ny, tensor)

    def at_z(d):
        return (dp, ((zl + d) % nzl) * 2 + core)

    y_order = sorted(range(1, ny), key=lambda d: -min(d, ny - d))
    x_order = sorted(range(1, nx), key=lambda d: -min(d, nx - d))
    def at_z_half(d):
        return (dp, ((zl // zhalf) * zhalf + (zl + d) % zhalf) * 2 + core)

    core_peer = (dp, zl * 2 + 1 - core)
    far_peer = ((x * 2 + 1 - zh) * ny + y, tensor)
    partners = [core_peer, far_peer, *[at_x((x + d) % nx) for d in range(1, nx)]]
    partners += [at_z(zhalf)] + [at_z_half(d) for d in range(1, zhalf)] + [at_y(d) for d in range(1, ny)]

    counts = {"local": 0, "remote": 0}
    remote = []

    def local_copy(src, dst):
        copy = pltpu.make_async_copy(src, dst, load_sem.at[counts["local"]])
        counts["local"] += 1
        copy.start()
        return copy

    def send(src, dst, device):
        index = counts["remote"]
        counts["remote"] += 1
        copy = pltpu.make_async_remote_copy(
            src_ref=src,
            dst_ref=dst,
            send_sem=send_sem.at[index],
            recv_sem=recv_sem.at[index],
            device_id=device,
            device_id_type=MESH,
        )
        copy.start()
        remote.append(copy)
        return copy

    load_act = local_copy(act, act_v)
    load_pp = local_copy(proj.at[pl.ds(pl.multiple_of(tensor * cfg.feat, cfg.feat), cfg.feat)], pp_v)
    barrier = pltpu.get_barrier_semaphore()
    for partner in partners:
        pl.semaphore_signal(barrier, inc=1, device_id=partner, device_id_type=MESH)
    out_rows = pr_v.shape[0]
    load_pr = local_copy(proj.at[pl.ds(pl.multiple_of(dp * out_rows, out_rows), out_rows)], pr_v)
    load_m = [local_copy(m1, mm.at[zh, 0]), local_copy(m2, mm.at[zh, 1])]
    load_g = []
    for which, ref in enumerate((gg, gu)):
        for h in range(2):
            load_g.append(
                local_copy(ref.at[:, pl.ds(h * half, half)], g_v.at[which, pl.ds(h * cfg.tok, cfg.tok)])
            )

    load_act.wait()
    load_pp.wait()
    part = dot(act_v[...], pp_v[...])
    part_v[...] = part.reshape(2, htok, cfg.rank)
    csend[...] = part_v[1 - core].astype(BF16)
    sel_v[...] = row_select(cfg)
    for copy in load_m:
        copy.wait()

    pl.semaphore_wait(barrier, len(partners))

    to_core = send(csend, crecv, core_peer)
    load_pr.wait()
    rows_wide = dot_nt(pr_v[...], sel_v[...])
    lane_half = lax.shift_right_logical(lax.broadcasted_iota(jnp.int32, rows_wide.shape, 1), 2) & 1
    for h in range(2):
        pw_v[h] = jnp.where(lane_half == h, rows_wide, 0.0).astype(BF16)
    save_pw = local_copy(pw_v, pw_out)
    to_core.wait_recv()
    mine = part_v[core] + crecv[...].astype(F32)
    zsend[...] = mine.astype(BF16)
    part_v[core] = mine
    across = send(zsend, zrecv.at[0], at_z(zhalf))
    for copy in load_g:
        copy.wait()
    across.wait_recv()
    pair = part_v[core] + zrecv[0].astype(F32)
    zpair[...] = pair.astype(BF16)
    part_v[core] = pair
    to_chips = [send(zpair, zrecv.at[d], at_z_half(d)) for d in range(zhalf - 1, 0, -1)]
    for copy in to_chips:
        copy.wait_recv()
    total = part_v[core]
    for d in range(1, zhalf):
        total = total + zrecv[d].astype(F32)
    basis_v[core] = total.astype(BF16)
    finished = send(basis_v.at[core], basis_v.at[core], core_peer)
    finished.wait_recv()

    basis = basis_v[...].reshape(cfg.tok, cfg.rank)
    basis_wide = dot_nt(sel_v[...], basis)
    sub_half = lax.shift_right_logical(lax.broadcasted_iota(jnp.int32, basis_wide.shape, 0), 2) & 1
    for h in range(2):
        w_v[:, h * cfg.tok : (h + 1) * cfg.tok] = jnp.where(sub_half == h, basis_wide, 0.0).astype(BF16)

    def block(xblock):
        return pl.ds(xblock * ny, ny)

    first = []
    for k, (which, start, width) in enumerate(cfg.chunks):
        p, rx = bufs["p"][k], bufs["rx"][k]
        grads = g_v[which, :, start : start + width]
        p[...] = dot(w_v[...], grads).astype(BF16).reshape(cfg.pieces, 8, width)
        first.append([send(p.at[block((x + d) % nx)], rx.at[d - 1], at_x((x + d) % nx)) for d in x_order])

    moments = send(mm.at[zh], mm.at[zh], far_peer)

    third = []
    for k in range(nk):
        p, rx, sy, ry = (bufs[name][k] for name in ("p", "rx", "sy", "ry"))
        for copy in first[k]:
            copy.wait_recv()
        own = p[block(x)].astype(F32)
        for d in range(1, nx):
            own = own + rx[d - 1].astype(F32)
        sy[...] = own.astype(BF16)
        third.append([send(sy.at[(y + d) % ny], ry.at[d - 1], at_y(d)) for d in y_order])

    moments.wait_recv()
    for moment in range(2):
        for end in range(2):
            for j in range(2):
                for which in range(2):
                    for h in range(2):
                        ml[moment, pl.ds(4 * h + 2 * end + j, 1), pl.ds(which * half, half)] = mm[
                            end, moment, j, pl.ds(which, 1), pl.ds(h * half, half)
                        ]

    fourth = []
    for k in range(nk):
        sy, ry, sz, rz, tf = (bufs[name][k] for name in ("sy", "ry", "sz", "rz", "tf"))
        for copy in third[k]:
            copy.wait_recv()
        total = sy[y].astype(F32)
        for d in range(1, ny):
            total = total + ry[d - 1].astype(F32)
        tf[...] = total
        sz[...] = total.astype(BF16)
        fourth.append(send(sz, rz, far_peer))

    corr_one = 1.0 - 0.9**STEP
    corr_two = 1.0 - 0.999**STEP
    fifth = []
    for k, (which, start, width) in enumerate(cfg.chunks):
        rz, tf, g = (bufs[name][k] for name in ("rz", "tf", "g"))
        fourth[k].wait_recv()
        cols = pl.ds(which * half + start, width)
        grad = tf[...] + rz[...].astype(F32)
        new_first = 0.9 * ml[0, :, cols] + 0.1 * grad
        new_second = 0.999 * ml[1, :, cols] + 0.001 * grad * grad
        step = new_first / corr_one / (jnp.sqrt(new_second / corr_two) + 1e-08)
        g[x * ny + y] = step.astype(BF16)
        fifth.append([send(g.at[x * ny + y], g.at[x * ny + y], at_y(d)) for d in y_order])
        nfl[:, cols] = new_first
        nsl[:, cols] = new_second

    sixth = []
    for k in range(nk):
        g = bufs["g"][k]
        for copy in fifth[k]:
            copy.wait_recv()
        own = block(x)
        sixth.append([send(g.at[own], g.at[own], at_x((x + d) % nx)) for d in x_order])

    for j in range(2):
        for which in range(2):
            for h in range(2):
                for flat, out in ((nfl, nf_out), (nsl, ns_out)):
                    out[j, pl.ds(which, 1), pl.ds(h * half, half)] = flat[
                        pl.ds(4 * h + j + 2 * zh, 1), pl.ds(which * half, half)
                    ]

    for k in range(nk):
        for copy in sixth[k]:
            copy.wait_recv()
    for copy in remote:
        copy.wait_send()
    save_pw.wait()


def update_kernel(cfg, *refs):
    nk = len(cfg.chunks)
    gs, refs = refs[:nk], refs[nk:]
    pw, nf, ns, gate, up, nf_out, ns_out, refs = *refs[:7], refs[7:]
    out_vs, (sem,) = refs[:nk], refs[nk:]
    saves = []
    for k, (which, start, width) in enumerate(cfg.chunks):
        steps = gs[k][...].reshape(cfg.pieces * 8, width)
        for h in range(2):
            out_vs[k][h] = dot(pw[h], steps).astype(BF16)
            columns = pl.ds(h * cfg.half + start, width)
            copy = pltpu.make_async_copy(
                out_vs[k].at[h], (gate, up)[which].at[:, columns], sem.at[2 * k + h]
            )
            copy.start()
            saves.append(copy)
    nf_out[...] = nf[...]
    ns_out[...] = ns[...]
    for copy in saves:
        copy.wait()


def shards(cfg, *inputs):
    _, projection, _, _, first_moment, _ = inputs
    nk = len(cfg.chunks)
    out_rows = projection.shape[0] // (2 * cfg.pieces)
    wide, htok = cfg.pieces * 8, cfg.tok // 2
    any_spec = pl.BlockSpec(memory_space=pl.ANY)
    vmem_spec = pl.BlockSpec(memory_space=pltpu.VMEM)
    small = jax.ShapeDtypeStruct(first_moment.shape, F32)

    def chunked(*shape, dtype=BF16):
        return [pltpu.VMEM((*shape, width), dtype) for width in cfg.widths]

    remote_copies = 3 + cfg.nzl // 2 + nk * (2 * (cfg.nx - 1) + 2 * (cfg.ny - 1) + 1)
    scratch = [
        pltpu.VMEM((cfg.tok, cfg.feat), BF16),
        pltpu.VMEM((cfg.feat, cfg.rank), BF16),
        pltpu.VMEM((2, 2 * cfg.tok, cfg.half), BF16),
        pltpu.VMEM((out_rows, cfg.rank), BF16),
        pltpu.VMEM((wide, cfg.rank), BF16),
        pltpu.VMEM((2, out_rows, wide), BF16),
        pltpu.VMEM((wide, 2 * cfg.tok), BF16),
        pltpu.VMEM((2, 2, 2, 2, cfg.ff), F32),
        pltpu.VMEM((2, 8, cfg.ff), F32),
        pltpu.VMEM((8, cfg.ff), F32),
        pltpu.VMEM((8, cfg.ff), F32),
        pltpu.VMEM((2, htok, cfg.rank), F32),
        pltpu.VMEM((htok, cfg.rank), BF16),
        pltpu.VMEM((htok, cfg.rank), BF16),
        pltpu.VMEM((htok, cfg.rank), BF16),
        pltpu.VMEM((htok, cfg.rank), BF16),
        pltpu.VMEM((cfg.nzl // 2, htok, cfg.rank), BF16),
        pltpu.VMEM((2, htok, cfg.rank), BF16),
        *chunked(cfg.pieces, 8),
        *chunked(cfg.nx - 1, cfg.ny, 8),
        *chunked(cfg.ny, 8),
        *chunked(cfg.ny - 1, 8),
        *chunked(8),
        *chunked(8),
        *chunked(8, dtype=F32),
        pltpu.SemaphoreType.DMA((10,)),
        pltpu.SemaphoreType.DMA((remote_copies,)),
        pltpu.SemaphoreType.DMA((remote_copies,)),
    ]
    gathered = chunked(cfg.pieces, 8)
    *steps, rows_wide, new_first, new_second = pl.pallas_call(
        functools.partial(comm_kernel, cfg),
        out_shape=(*gathered, jax.ShapeDtypeStruct((2, out_rows, wide), BF16), small, small),
        in_specs=[pl.BlockSpec(memory_space=pltpu.HBM)] * 6,
        out_specs=(*[vmem_spec] * nk, any_spec, vmem_spec, vmem_spec),
        scratch_shapes=scratch,
        compiler_params=pltpu.CompilerParams(collective_id=0, has_side_effects=True, vmem_limit_bytes=48 << 20),
        name="comm",
    )(*[pltpu.with_memory_space_constraint(ref, pltpu.HBM) for ref in inputs])
    update = jax.ShapeDtypeStruct((out_rows, cfg.ff), BF16)
    return pl.pallas_call(
        functools.partial(update_kernel, cfg),
        out_shape=(update, update, small, small),
        in_specs=[vmem_spec] * (nk + 3),
        out_specs=(any_spec, any_spec, vmem_spec, vmem_spec),
        scratch_shapes=[
            *chunked(2, out_rows),
            pltpu.SemaphoreType.DMA((2 * nk,)),
        ],
        compiler_params=pltpu.CompilerParams(vmem_limit_bytes=48 << 20),
        name="update",
    )(*steps, rows_wide, new_first, new_second)


def build(mesh, cfg):
    in_specs = (
        P("dp", "tensor"),
        P(),
        P("dp", "tensor"),
        P("dp", "tensor"),
        P("dp", None, "tensor"),
        P("dp", None, "tensor"),
    )
    out_specs = (
        P("dp", "tensor"),
        P("dp", "tensor"),
        P("dp", None, "tensor"),
        P("dp", None, "tensor"),
    )
    return jax.shard_map(
        functools.partial(shards, cfg), mesh=mesh, in_specs=in_specs, out_specs=out_specs, check_vma=False
    )


def solution(mesh):
    return build(mesh, Cfg(ny=8, nzl=8, tok=128, feat=512, ff=1792, chunks=((0, 0, 384), (0, 384, 512), (1, 0, 512), (1, 512, 256), (1, 768, 128))))
```

```python
import dataclasses
import functools

import jax
import jax.numpy as jnp
from jax import lax
from jax.experimental import pallas as pl
from jax.experimental.pallas import tpu as pltpu
from jax.sharding import PartitionSpec as P

STEP = 1000
BF16 = jnp.bfloat16
F32 = jnp.float32
MESH = pl.DeviceIdType.MESH


@dataclasses.dataclass(frozen=True)
class Cfg:
    ny: int
    nzl: int
    tok: int
    feat: int
    ff: int
    chunks: tuple
    nx: int = 4

    @property
    def pieces(self):
        return self.nx * self.ny

    @property
    def rank(self):
        return 4 * self.pieces

    @property
    def half(self):
        return self.ff // 2

    @property
    def widths(self):
        return [width for _, _, width in self.chunks]


def row_select(cfg):
    shape = (cfg.pieces, 8, cfg.rank)
    piece = lax.broadcasted_iota(jnp.int32, shape, 0)
    sub = lax.broadcasted_iota(jnp.int32, shape, 1)
    row = lax.broadcasted_iota(jnp.int32, shape, 2)
    ybits = cfg.ny.bit_length() - 1
    px = lax.shift_right_logical(piece, ybits)
    py = piece & (cfg.ny - 1)
    zh = lax.shift_right_logical(sub, 1) & 1
    target = (px * 2 + zh) * (2 * cfg.ny) + py * 2 + (sub & 1)
    return jnp.where(row == target, 1.0, 0.0).astype(BF16).reshape(cfg.pieces * 8, cfg.rank)


def dot(a, b):
    return jnp.dot(a, b, preferred_element_type=F32)


def dot_nt(a, b):
    return lax.dot_general(a, b, (((1,), (1,)), ((), ())), preferred_element_type=F32)


def comm_kernel(cfg, *refs):
    nk = len(cfg.chunks)
    nx, ny, nzl, half = cfg.nx, cfg.ny, cfg.nzl, cfg.half
    zhalf, htok = nzl // 2, cfg.tok // 2
    (act, proj, gg, gu, m1, m2), refs = refs[:6], refs[6:]
    g_outs, refs = refs[:nk], refs[nk:]
    (pw_out, nf_out, ns_out), refs = refs[:3], refs[3:]
    (act_v, pp_v, g_v, pr_v, sel_v, pw_v, w_v, mm, ml, nfl, nsl), refs = refs[:11], refs[11:]
    (part_v, psend, precv, zpair, zrecv, basis_v), refs = refs[:6], refs[6:]
    names = ("p", "rx", "sy", "ry", "sz", "rz", "tf")
    bufs = {"g": g_outs}
    for name in names:
        bufs[name], refs = refs[:nk], refs[nk:]
    load_sem, send_sem, recv_sem = refs

    dp, tensor = lax.axis_index("dp"), lax.axis_index("tensor")
    core, zl = tensor % 2, tensor // 2
    y, zh, x = dp % ny, (dp // ny) % 2, dp // (2 * ny)

    def at_x(other):
        return ((other * 2 + zh) * ny + y, tensor)

    def at_y(d):
        return ((x * 2 + zh) * ny + (y + d) % ny, tensor)

    def at_z(d, other):
        return (dp, ((zl + d) % nzl) * 2 + other)

    y_order = sorted(range(1, ny), key=lambda d: -min(d, ny - d))
    x_order = sorted(range(1, nx), key=lambda d: -min(d, nx - d))
    def at_z_half(d, other):
        return (dp, ((zl // zhalf) * zhalf + (zl + d) % zhalf) * 2 + other)

    core_peer = (dp, zl * 2 + 1 - core)
    far_peer = ((x * 2 + 1 - zh) * ny + y, tensor)
    partners = [core_peer, far_peer, *[at_x((x + d) % nx) for d in range(1, nx)]]
    cores = (core, 1 - core)
    partners += [at_z(zhalf, other) for other in cores]
    partners += [at_z_half(d, other) for d in range(1, zhalf) for other in cores]
    partners += [at_y(d) for d in range(1, ny)]

    counts = {"local": 0, "remote": 0}
    remote = []

    def local_copy(src, dst):
        copy = pltpu.make_async_copy(src, dst, load_sem.at[counts["local"]])
        counts["local"] += 1
        copy.start()
        return copy

    def send(src, dst, device):
        index = counts["remote"]
        counts["remote"] += 1
        copy = pltpu.make_async_remote_copy(
            src_ref=src,
            dst_ref=dst,
            send_sem=send_sem.at[index],
            recv_sem=recv_sem.at[index],
            device_id=device,
            device_id_type=MESH,
        )
        copy.start()
        remote.append(copy)
        return copy

    load_act = local_copy(act, act_v)
    load_pp = local_copy(proj.at[pl.ds(pl.multiple_of(tensor * cfg.feat, cfg.feat), cfg.feat)], pp_v)
    barrier = pltpu.get_barrier_semaphore()
    for partner in partners:
        pl.semaphore_signal(barrier, inc=1, device_id=partner, device_id_type=MESH)
    out_rows = pr_v.shape[0]
    load_pr = local_copy(proj.at[pl.ds(pl.multiple_of(dp * out_rows, out_rows), out_rows)], pr_v)
    load_m = [local_copy(m1, mm.at[zh, 0]), local_copy(m2, mm.at[zh, 1])]
    load_g = []
    for which, ref in enumerate((gg, gu)):
        for h in range(2):
            load_g.append(
                local_copy(ref.at[:, pl.ds(h * half, half)], g_v.at[which, pl.ds(h * cfg.tok, cfg.tok)])
            )

    load_act.wait()
    load_pp.wait()
    part = dot(act_v[...], pp_v[...])
    part_v[...] = part.reshape(2, htok, cfg.rank)
    psend[...] = part_v[...].astype(BF16)
    sel_v[...] = row_select(cfg)
    for copy in load_m:
        copy.wait()

    pl.semaphore_wait(barrier, len(partners))

    near = [
        send(psend.at[core], precv.at[0], at_z(zhalf, core)),
        send(psend.at[1 - core], precv.at[1], at_z(zhalf, 1 - core)),
        send(psend.at[1 - core], precv.at[2], core_peer),
    ]
    load_pr.wait()
    rows_wide = dot_nt(pr_v[...], sel_v[...])
    lane_half = lax.shift_right_logical(lax.broadcasted_iota(jnp.int32, rows_wide.shape, 1), 2) & 1
    for h in range(2):
        pw_v[h] = jnp.where(lane_half == h, rows_wide, 0.0).astype(BF16)
    save_pw = local_copy(pw_v, pw_out)
    for copy in near:
        copy.wait_recv()
    pair = part_v[core] + (precv[0].astype(F32) + precv[1].astype(F32) + precv[2].astype(F32))
    zpair[...] = pair.astype(BF16)
    part_v[core] = pair
    to_chips = []
    for d in range(zhalf - 1, 0, -1):
        for mine, other in enumerate(cores):
            to_chips.append(send(zpair, zrecv.at[mine, d], at_z_half(d, other)))
    to_chips.append(send(zpair, zrecv.at[1, 0], core_peer))
    for copy in load_g:
        copy.wait()
    for copy in to_chips:
        copy.wait_recv()
    total = part_v[core]
    for d in range(1, zhalf):
        total = total + zrecv[0, d].astype(F32)
    basis_v[core] = total.astype(BF16)
    total = zrecv[1, 0].astype(F32)
    for d in range(1, zhalf):
        total = total + zrecv[1, d].astype(F32)
    basis_v[1 - core] = total.astype(BF16)

    basis = basis_v[...].reshape(cfg.tok, cfg.rank)
    basis_wide = dot_nt(sel_v[...], basis)
    sub_half = lax.shift_right_logical(lax.broadcasted_iota(jnp.int32, basis_wide.shape, 0), 2) & 1
    for h in range(2):
        w_v[:, h * cfg.tok : (h + 1) * cfg.tok] = jnp.where(sub_half == h, basis_wide, 0.0).astype(BF16)

    def block(xblock):
        return pl.ds(xblock * ny, ny)

    first = []
    for k, (which, start, width) in enumerate(cfg.chunks):
        p, rx = bufs["p"][k], bufs["rx"][k]
        grads = g_v[which, :, start : start + width]
        p[...] = dot(w_v[...], grads).astype(BF16).reshape(cfg.pieces, 8, width)
        first.append([send(p.at[block((x + d) % nx)], rx.at[d - 1], at_x((x + d) % nx)) for d in x_order])

    moments = send(mm.at[zh], mm.at[zh], far_peer)

    third = []
    for k in range(nk):
        p, rx, sy, ry = (bufs[name][k] for name in ("p", "rx", "sy", "ry"))
        for copy in first[k]:
            copy.wait_recv()
        own = p[block(x)].astype(F32)
        for d in range(1, nx):
            own = own + rx[d - 1].astype(F32)
        sy[...] = own.astype(BF16)
        third.append([send(sy.at[(y + d) % ny], ry.at[d - 1], at_y(d)) for d in y_order])

    moments.wait_recv()
    for moment in range(2):
        for end in range(2):
            for j in range(2):
                for which in range(2):
                    for h in range(2):
                        ml[moment, pl.ds(4 * h + 2 * end + j, 1), pl.ds(which * half, half)] = mm[
                            end, moment, j, pl.ds(which, 1), pl.ds(h * half, half)
                        ]

    fourth = []
    for k in range(nk):
        sy, ry, sz, rz, tf = (bufs[name][k] for name in ("sy", "ry", "sz", "rz", "tf"))
        for copy in third[k]:
            copy.wait_recv()
        total = sy[y].astype(F32)
        for d in range(1, ny):
            total = total + ry[d - 1].astype(F32)
        tf[...] = total
        sz[...] = total.astype(BF16)
        fourth.append(send(sz, rz, far_peer))

    corr_one = 1.0 - 0.9**STEP
    corr_two = 1.0 - 0.999**STEP
    fifth = []
    for k, (which, start, width) in enumerate(cfg.chunks):
        rz, tf, g = (bufs[name][k] for name in ("rz", "tf", "g"))
        fourth[k].wait_recv()
        cols = pl.ds(which * half + start, width)
        grad = tf[...] + rz[...].astype(F32)
        new_first = 0.9 * ml[0, :, cols] + 0.1 * grad
        new_second = 0.999 * ml[1, :, cols] + 0.001 * grad * grad
        step = new_first / corr_one / (jnp.sqrt(new_second / corr_two) + 1e-08)
        g[x * ny + y] = step.astype(BF16)
        fifth.append([send(g.at[x * ny + y], g.at[x * ny + y], at_y(d)) for d in y_order])
        nfl[:, cols] = new_first
        nsl[:, cols] = new_second

    sixth = []
    for k in range(nk):
        g = bufs["g"][k]
        for copy in fifth[k]:
            copy.wait_recv()
        own = block(x)
        sixth.append([send(g.at[own], g.at[own], at_x((x + d) % nx)) for d in x_order])

    for j in range(2):
        for which in range(2):
            for h in range(2):
                for flat, out in ((nfl, nf_out), (nsl, ns_out)):
                    out[j, pl.ds(which, 1), pl.ds(h * half, half)] = flat[
                        pl.ds(4 * h + j + 2 * zh, 1), pl.ds(which * half, half)
                    ]

    for k in range(nk):
        for copy in sixth[k]:
            copy.wait_recv()
    for copy in remote:
        copy.wait_send()
    save_pw.wait()


def update_kernel(cfg, *refs):
    nk = len(cfg.chunks)
    gs, refs = refs[:nk], refs[nk:]
    pw, nf, ns, gate, up, nf_out, ns_out, refs = *refs[:7], refs[7:]
    out_vs, (sem,) = refs[:nk], refs[nk:]
    saves = []
    for k, (which, start, width) in enumerate(cfg.chunks):
        steps = gs[k][...].reshape(cfg.pieces * 8, width)
        for h in range(2):
            out_vs[k][h] = dot(pw[h], steps).astype(BF16)
            columns = pl.ds(h * cfg.half + start, width)
            copy = pltpu.make_async_copy(
                out_vs[k].at[h], (gate, up)[which].at[:, columns], sem.at[2 * k + h]
            )
            copy.start()
            saves.append(copy)
    nf_out[...] = nf[...]
    ns_out[...] = ns[...]
    for copy in saves:
        copy.wait()


def shards(cfg, *inputs):
    _, projection, _, _, first_moment, _ = inputs
    nk = len(cfg.chunks)
    out_rows = projection.shape[0] // (2 * cfg.pieces)
    wide, htok = cfg.pieces * 8, cfg.tok // 2
    any_spec = pl.BlockSpec(memory_space=pl.ANY)
    vmem_spec = pl.BlockSpec(memory_space=pltpu.VMEM)
    small = jax.ShapeDtypeStruct(first_moment.shape, F32)

    def chunked(*shape, dtype=BF16):
        return [pltpu.VMEM((*shape, width), dtype) for width in cfg.widths]

    remote_copies = 3 + cfg.nzl + nk * (2 * (cfg.nx - 1) + 2 * (cfg.ny - 1) + 1)
    scratch = [
        pltpu.VMEM((cfg.tok, cfg.feat), BF16),
        pltpu.VMEM((cfg.feat, cfg.rank), BF16),
        pltpu.VMEM((2, 2 * cfg.tok, cfg.half), BF16),
        pltpu.VMEM((out_rows, cfg.rank), BF16),
        pltpu.VMEM((wide, cfg.rank), BF16),
        pltpu.VMEM((2, out_rows, wide), BF16),
        pltpu.VMEM((wide, 2 * cfg.tok), BF16),
        pltpu.VMEM((2, 2, 2, 2, cfg.ff), F32),
        pltpu.VMEM((2, 8, cfg.ff), F32),
        pltpu.VMEM((8, cfg.ff), F32),
        pltpu.VMEM((8, cfg.ff), F32),
        pltpu.VMEM((2, htok, cfg.rank), F32),
        pltpu.VMEM((2, htok, cfg.rank), BF16),
        pltpu.VMEM((3, htok, cfg.rank), BF16),
        pltpu.VMEM((htok, cfg.rank), BF16),
        pltpu.VMEM((2, cfg.nzl // 2, htok, cfg.rank), BF16),
        pltpu.VMEM((2, htok, cfg.rank), BF16),
        *chunked(cfg.pieces, 8),
        *chunked(cfg.nx - 1, cfg.ny, 8),
        *chunked(cfg.ny, 8),
        *chunked(cfg.ny - 1, 8),
        *chunked(8),
        *chunked(8),
        *chunked(8, dtype=F32),
        pltpu.SemaphoreType.DMA((10,)),
        pltpu.SemaphoreType.DMA((remote_copies,)),
        pltpu.SemaphoreType.DMA((remote_copies,)),
    ]
    gathered = chunked(cfg.pieces, 8)
    *steps, rows_wide, new_first, new_second = pl.pallas_call(
        functools.partial(comm_kernel, cfg),
        out_shape=(*gathered, jax.ShapeDtypeStruct((2, out_rows, wide), BF16), small, small),
        in_specs=[pl.BlockSpec(memory_space=pltpu.HBM)] * 6,
        out_specs=(*[vmem_spec] * nk, any_spec, vmem_spec, vmem_spec),
        scratch_shapes=scratch,
        compiler_params=pltpu.CompilerParams(collective_id=0, has_side_effects=True, vmem_limit_bytes=48 << 20),
        name="comm",
    )(*[pltpu.with_memory_space_constraint(ref, pltpu.HBM) for ref in inputs])
    update = jax.ShapeDtypeStruct((out_rows, cfg.ff), BF16)
    return pl.pallas_call(
        functools.partial(update_kernel, cfg),
        out_shape=(update, update, small, small),
        in_specs=[vmem_spec] * (nk + 3),
        out_specs=(any_spec, any_spec, vmem_spec, vmem_spec),
        scratch_shapes=[
            *chunked(2, out_rows),
            pltpu.SemaphoreType.DMA((2 * nk,)),
        ],
        compiler_params=pltpu.CompilerParams(vmem_limit_bytes=48 << 20),
        name="update",
    )(*steps, rows_wide, new_first, new_second)


def build(mesh, cfg):
    in_specs = (
        P("dp", "tensor"),
        P(),
        P("dp", "tensor"),
        P("dp", "tensor"),
        P("dp", None, "tensor"),
        P("dp", None, "tensor"),
    )
    out_specs = (
        P("dp", "tensor"),
        P("dp", "tensor"),
        P("dp", None, "tensor"),
        P("dp", None, "tensor"),
    )
    return jax.shard_map(
        functools.partial(shards, cfg), mesh=mesh, in_specs=in_specs, out_specs=out_specs, check_vma=False
    )


def solution(mesh):
    return build(mesh, Cfg(ny=8, nzl=8, tok=128, feat=512, ff=1792, chunks=((0, 0, 384), (0, 384, 512), (1, 0, 512), (1, 512, 256), (1, 768, 128))))
```
